32 devices in a mesh: lon: 16 (over z, x, core), mem: 2 (over y).
Axes of the slice: x: 2, y: 2, z: 4, core: 2. Of those that a mesh axis runs over, the one named last changes fastest.
Arguments:
- ensemble: bfloat16 [128, 6, 524288], P('mem', None, 'lon'), may hold values from -6 to 6
- control: float32 [128, 524288], P('mem', 'lon'), may hold values from -6 to 6
- obs_tiles: bfloat16 [2048, 128, 128], P('lon'), as said below
- innovation: float32 [2048, 128], P('lon'), may hold values from -6 to 6
- obs_weight: float32 [2048, 128], P('lon'), may hold values from 0.25 to 4
- obs_counts: int32 [2048], P('lon'), may hold values from 16 to 128, as said below
- node_blocks: int32 [2048], replicated, may hold values from 0 to 4095, as said below
- obs_slots: int32 [2048], replicated, may hold values from 0 to 5
Outputs:
- gradient: float32 [128, 524288], P('mem', 'lon')
The draws below stay inside these ranges and needn't reach their ends.
Inputs may be any that keep to these rules, and one draw needn't show every extreme that they name: `node_blocks`: within the entries of one owner (aligned runs of 128), at most 8 name node blocks of one lon index (blocks d * 256 to (d + 1) * 256 - 1); in every draw some owner names exactly 8 of one lon index. `obs_counts`: some block in every draw is full. `obs_tiles`: each tile has a positive diagonal plus off-diagonal entries.
All inputs are finite; a program needn't handle non-finite values.
Results may differ from the reference program's by a relative error of at most 0.0003.
Values sent between devices are 32-bit elements; how exact they have to be, the bound alone decides.
A program may use at most 192 MiB of HBM per device.

```python
import math
import jax
import jax.numpy as jnp
from jax import lax

MEMBERS = 128
SLOTS = 6
BLOCK = 128
BLK_DEV = 256
OBS_DEV = 128
CAP = 8
NODE_BLOCKS = 4096
NODES = 524288
OBS_BLOCKS = 2048
N_LON = 16


def draw_node_blocks(key, part):
    slot_total = N_LON * CAP
    coastal = jax.random.randint(jax.random.fold_in(key, 5), (N_LON,), 0, 4) == 0
    anchor = jax.random.randint(jax.random.fold_in(key, 6), (), 0, N_LON)

    def one_owner(owner_dev):
        owner_key = jax.random.fold_in(key, owner_dev + 100)
        shuffled = jax.random.permutation(owner_key, slot_total)
        target = shuffled // CAP
        priority = jnp.arange(slot_total) - slot_total * coastal[target].astype(jnp.int32) - 2 * slot_total * (target == anchor).astype(jnp.int32)
        ordering = jnp.argsort(priority)
        chosen = shuffled[ordering][:OBS_DEV] // CAP
        local_blk = jax.random.randint(jax.random.fold_in(owner_key, 3), (OBS_DEV,), 0, BLK_DEV)
        return chosen * BLK_DEV + local_blk
    return jax.vmap(one_owner)(jnp.arange(N_LON)).reshape(N_LON * OBS_DEV).astype(jnp.int32)


def draw_obs_counts(key, part):
    drawn = jax.random.randint(key, (N_LON * OBS_DEV,), BLOCK // 8, BLOCK + 1)
    return drawn.at[0].set(BLOCK).astype(jnp.int32)


def draw_obs_tiles(key, part):
    first_key = jax.random.fold_in(key, 1)
    second_key = jax.random.fold_in(key, 2)
    shape_all = (N_LON * OBS_DEV, BLOCK, BLOCK)
    random_part = jax.random.normal(first_key, shape_all, jnp.float32) / math.sqrt(BLOCK)
    diagonal = 1.0 + jax.random.uniform(second_key, (N_LON * OBS_DEV, BLOCK), jnp.float32)
    identity = jnp.eye(BLOCK, dtype=jnp.float32)
    return (random_part + identity[None, :, :] * diagonal[:, :, None]).astype(jnp.bfloat16)


def set_ends(array, stream_key, smallest, high):
    longest = array.shape.index(max(array.shape))
    spots = []
    for shift in (0, 1):
        where = [jax.random.randint(jax.random.fold_in(stream_key, axis), (), 0, length) for axis, length in enumerate(array.shape)]
        where[longest] = (where[longest] + shift) % array.shape[longest]
        spots.append(tuple(where))
    return array.at[spots[0]].set(smallest).at[spots[1]].set(high)


def shard_levels(rng, dims, shards, least, largest):
    level, own = 1.0, jax.random.fold_in(rng, 6)
    for position, shards_of in shards:
        steps = jnp.exp(jax.random.uniform(jax.random.fold_in(own, position), (shards_of,), jnp.float32, least / len(shards), largest / len(shards)))
        level = level * jnp.repeat(steps, dims[position] // shards_of).reshape([-1 if axis == position else 1 for axis in range(len(dims))])
    return level


def scatter_about(rng, extent, spread, limit, pieces=(), kind=jnp.bfloat16):
    level = shard_levels(rng, extent, pieces, -0.22, 0.18) if pieces else 1.0
    values = jax.random.normal(rng, extent, jnp.float32) * spread * level
    return jnp.minimum(jnp.maximum(values, -limit), limit).astype(kind)


def setup_inputs(seed: int = 0) -> dict:
    key_of = jax.random.split(jax.random.key(seed), 9)
    ensemble = scatter_about(key_of[0], (MEMBERS, SLOTS, NODES), 1.0, 6.0, ((0, 2), (2, 16)))
    control = scatter_about(key_of[1], (MEMBERS, NODES), 1.0, 6.0, ((0, 2), (1, 16)), jnp.float32)
    obs_tiles = draw_obs_tiles(jax.random.fold_in(key_of[8], 71), 0)
    innovation = scatter_about(key_of[3], (OBS_BLOCKS, BLOCK), 1.0, 6.0, ((0, 16),), jnp.float32)
    obs_weight = jnp.clip(jnp.exp(math.log(4.0) - 2.7725887 * jax.random.uniform(key_of[4], (OBS_BLOCKS, BLOCK), jnp.float32) ** shard_levels(key_of[4], (OBS_BLOCKS, BLOCK), ((0, 16),), -0.2, 0.2)), 0.25, 4.0)
    obs_counts = draw_obs_counts(jax.random.fold_in(key_of[8], 71), 0)
    node_blocks = draw_node_blocks(jax.random.fold_in(key_of[8], 71), 0)
    obs_slots = set_ends(jax.random.randint(key_of[7], (OBS_BLOCKS,), 0, SLOTS), jax.random.fold_in(key_of[7], 1), 0, SLOTS - 1).astype(jnp.int32)
    return {"ensemble": ensemble, "control": control, "obs_tiles": obs_tiles, "innovation": innovation, "obs_weight": obs_weight, "obs_counts": obs_counts, "node_blocks": node_blocks, "obs_slots": obs_slots}


def kernel_tables(blk_size):
    lag_base = jnp.arange(blk_size)[:, None] - jnp.arange(blk_size)[None, :]
    all_lags = jnp.arange(-blk_size, blk_size + 1).astype(jnp.float32)
    norm_sq = jnp.sum(jnp.exp(-(3.0 * all_lags / blk_size) ** 2))
    tables = []
    for shift_index in range(3):
        lag_cells = (lag_base + (shift_index - 1) * blk_size).astype(jnp.float32)
        raw_values = jnp.where(jnp.abs(lag_cells) <= blk_size, jnp.exp(-0.5 * (3.0 * lag_cells / blk_size) ** 2), 0.0)
        tables.append(raw_values / jnp.sqrt(norm_sq))
    return jnp.stack(tables)

def smooth(values_in, blk_size):
    row_count, width_cells = values_in.shape
    block_count = width_cells // blk_size
    padded = jnp.concatenate([values_in[:, width_cells - blk_size:], values_in, values_in[:, :blk_size]], axis=1)
    blocks = padded.reshape(row_count, block_count + 2, blk_size)
    tables = kernel_tables(blk_size)
    summed = jnp.zeros((row_count, block_count, blk_size), jnp.float32)
    for shift_index in range(3):
        summed = summed + jnp.einsum('rbi,io->rbo', blocks[:, shift_index:shift_index + block_count], tables[shift_index], precision=lax.Precision.HIGHEST)
    return summed.reshape(row_count, width_cells)

def reference(ensemble, control, obs_tiles, innovation, obs_weight, obs_counts, node_blocks, obs_slots):
    scaling = 1.0 / jnp.sqrt(jnp.float32(MEMBERS - 1))
    weights = smooth(control, BLOCK)
    increment = jnp.stack([lax.optimization_barrier(jnp.sum(weights * ensemble[:, slot_index, :].astype(jnp.float32), axis=0)) for slot_index in range(SLOTS)]) * scaling
    layered = increment.reshape(SLOTS, NODE_BLOCKS, BLOCK)
    fetched = layered[obs_slots, node_blocks]
    tile_values = obs_tiles.astype(jnp.float32)
    observed = jnp.einsum('gon,gn->go', tile_values, fetched, precision=lax.Precision.HIGHEST)
    live_rows = jnp.arange(BLOCK)[None, :] < obs_counts[:, None]
    departure = jnp.where(live_rows, obs_weight * (observed - innovation), 0.0)
    adjoint_blocks = jnp.einsum('gon,go->gn', tile_values, departure, precision=lax.Precision.HIGHEST)
    adjoint = jnp.zeros((SLOTS, NODE_BLOCKS, BLOCK), jnp.float32).at[obs_slots, node_blocks].add(adjoint_blocks).reshape(SLOTS, NODES)
    weight_grad = jnp.zeros(control.shape, jnp.float32)
    for slot_index in range(SLOTS):
        weight_grad = weight_grad + ensemble[:, slot_index, :].astype(jnp.float32) * adjoint[slot_index][None, :]
    weight_grad = weight_grad * scaling
    return control + smooth(weight_grad, BLOCK)
```

```python
import functools
import math

import jax
import jax.numpy as jnp
import numpy as np
from jax import lax
from jax.experimental import pallas as pl
from jax.experimental.pallas import tpu as pltpu
from jax.sharding import PartitionSpec as P

CAP = 8
GROUP = 8
F32 = jnp.float32
BF16 = jnp.bfloat16
ANY = pl.BlockSpec(memory_space=pl.ANY)
VMEM = pl.BlockSpec(memory_space=pltpu.VMEM)
SMEM = pl.BlockSpec(memory_space=pltpu.SMEM)
LIMIT = 60 << 20


def params(**kw):
    return pltpu.CompilerParams(vmem_limit_bytes=LIMIT, **kw)


def tables(blk):
    lag = np.arange(blk)[:, None] - np.arange(blk)[None, :]
    every = np.arange(-blk, blk + 1)
    norm = np.sqrt(np.sum(np.exp(-((3.0 * every / blk) ** 2))))
    parts = []
    for shift in range(3):
        cells = lag + (shift - 1) * blk
        raw = np.where(np.abs(cells) <= blk, np.exp(-0.5 * (3.0 * cells / blk) ** 2), 0.0)
        parts.append(raw / norm)
    bf = jnp.bfloat16.dtype if hasattr(jnp.bfloat16, "dtype") else np.dtype(jnp.bfloat16)

    def halves(value):
        high = value.astype(np.float32).astype(bf)
        low = (value - high.astype(np.float64)).astype(np.float32).astype(bf)
        return high, low

    high, low = halves(np.concatenate(parts, axis=0))
    forward = np.concatenate(
        [
            np.concatenate([high, low], axis=1),
            np.concatenate([high, np.zeros_like(low)], axis=1),
        ],
        axis=0,
    )
    high, low = halves(np.concatenate(parts[::-1], axis=1))
    backward = np.concatenate(
        [
            np.concatenate([high, low], axis=1),
            np.concatenate([high, np.zeros_like(low)], axis=1),
        ],
        axis=0,
    )
    return forward, backward


def split(value):
    high = value.astype(BF16)
    return high, (value - high.astype(F32)).astype(BF16)


def index_kernel(nb, ranks, nodes_ref, slots_ref, code_ref, obs_ref):
    lon, obs = nodes_ref.shape
    my, mm = lax.axis_index("lon"), lax.axis_index("mem")
    tri = (
        lax.broadcasted_iota(jnp.int32, (obs, obs), 0)
        < lax.broadcasted_iota(jnp.int32, (obs, obs), 1)
    ).astype(F32).astype(BF16)
    lane = lax.broadcasted_iota(jnp.int32, (lon, 128), 1)

    def ranked(match):
        return jnp.dot(match.astype(F32).astype(BF16), tri, preferred_element_type=F32)

    local = nodes_ref[...] - my * nb
    match = (local >= 0) & (local < nb)
    rank = ranked(match)
    value = (slots_ref[...] * nb + local + 1).astype(F32)
    code = jnp.zeros((lon, 128), F32)
    for k in range(CAP):
        hit = match & (rank == float(k))
        code = jnp.where(lane == k, jnp.sum(jnp.where(hit, value, 0.0), axis=1, keepdims=True), code)
    code_ref[...] = code.astype(jnp.int32) - 1

    base = lax.broadcasted_iota(jnp.int32, (lon, obs), 0) * nb
    mine = nodes_ref[pl.ds(my, 1), :] - base
    match = (mine >= 0) & (mine < nb)
    rank = ranked(match) - (mm * ranks).astype(F32)
    value = (lax.broadcasted_iota(jnp.int32, (lon, obs), 1) + 1).astype(F32)
    which = jnp.zeros((lon, 128), F32)
    for r in range(ranks):
        hit = match & (rank == float(r))
        which = jnp.where(lane == r, jnp.sum(jnp.where(hit, value, 0.0), axis=1, keepdims=True), which)
    obs_ref[...] = which.astype(jnp.int32) - 1


def tile_copies(code_ref, ens_ref, buf, sems, nb, blk, groups):
    def start(g, carry):
        for k in range(GROUP):
            code = jnp.maximum(code_ref[g, k], 0)
            column = pl.multiple_of((code % nb) * blk, blk)
            pltpu.make_async_copy(
                ens_ref.at[code // nb, :, pl.ds(column, blk)], buf.at[g * GROUP + k], sems.at[g]
            ).start()
        return carry

    lax.fori_loop(0, groups, start, 0)


def wait_group(buf, sems, g):
    view = buf.at[pl.ds(g * GROUP, GROUP)]
    pltpu.make_async_copy(view, view, sems.at[g]).wait()


def row_copies(src, dst, sems, into):
    rows = src.shape[0]
    count = sems.shape[0]
    step = rows // count
    return [
        pltpu.make_async_copy(
            src.at[pl.ds(i * step, step), :], dst.at[pl.ds(i * step, step), into], sems.at[i]
        )
        for i in range(count)
    ]


def fetch_kernel(nb, blk, scaling, code_ref, before_ref, after_ref, table_ref, ctrl_ref, ens_ref,
                 out_ref, ext, buf, sems, row_sems):
    groups = code_ref.shape[0]
    members, nodes = ctrl_ref.shape
    copies = row_copies(ctrl_ref, ext, row_sems, pl.ds(blk, nodes))
    for copy in copies:
        copy.start()
    tile_copies(code_ref, ens_ref, buf, sems, nb, blk, groups)
    ext[:, :blk] = before_ref[...]
    ext[:, nodes + blk :] = after_ref[...]
    for copy in copies:
        copy.wait()

    def step(g, carry):
        pieces, live = [], []
        for k in range(GROUP):
            code = code_ref[g, k]
            live.append((code >= 0).astype(F32) * scaling)
            column = pl.multiple_of((jnp.maximum(code, 0) % nb) * blk, blk)
            pieces.append(ext[:, pl.ds(column, 3 * blk)])
        high, low = split(jnp.concatenate(pieces, axis=0))
        both = jnp.dot(
            jnp.concatenate([high, low], axis=1), table_ref[...], preferred_element_type=F32
        )
        weights = both[:, :blk] + both[:, blk:]
        wait_group(buf, sems, g)
        for k in range(GROUP):
            part = weights[k * members : (k + 1) * members] * buf[g * GROUP + k].astype(F32)
            out_ref[g, pl.ds(k, 1), :] = jnp.sum(part, axis=0, keepdims=True) * live[k]
        return carry

    lax.fori_loop(0, groups, step, 0)


def pair(row):
    high, low = split(row)
    index = lax.broadcasted_iota(jnp.int32, (16, row.shape[1]), 0)
    both = jnp.where(index == 0, high.astype(F32), jnp.where(index == 1, low.astype(F32), 0.0))
    return both.astype(BF16)


def observe_kernel(which_ref, counts_ref, got_ref, innov_ref, weight_ref, tiles_ref, out_ref,
                   buf, sems):
    lon, parts, ranks, blk = got_ref.shape

    def start(s, carry):
        for r in range(ranks):
            o = jnp.maximum(which_ref[s, r], 0)
            pltpu.make_async_copy(tiles_ref.at[o], buf.at[s * ranks + r], sems.at[s]).start()
        return carry

    lax.fori_loop(0, lon, start, 0)
    lane = lax.broadcasted_iota(jnp.int32, (1, blk), 1)
    together = 2 if lon % 2 == 0 else 1

    def step(i, carry):
        todo = []
        for j in range(together):
            s = i * together + j
            view = buf.at[pl.ds(s * ranks, ranks)]
            pltpu.make_async_copy(view, view, sems.at[s]).wait()
            rows = got_ref[s, 0]
            for part in range(1, parts):
                rows = rows + got_ref[s, part]
            for r in range(ranks):
                todo.append((s, r, rows[r : r + 1]))
        seen = [
            lax.dot_general(
                pair(row), buf[s * ranks + r], (((1,), (1,)), ((), ())), preferred_element_type=F32
            )
            for s, r, row in todo
        ]
        gaps = []
        for (s, r, _), value in zip(todo, seen):
            index = which_ref[s, r]
            o = jnp.maximum(index, 0)
            count = jnp.where(index >= 0, counts_ref[o], 0)
            observed = jnp.sum(value, axis=0, keepdims=True)
            gap = weight_ref[pl.ds(o, 1), :] * (observed - innov_ref[pl.ds(o, 1), :])
            gaps.append(jnp.where(lane < count, gap, 0.0))
        for (s, r, _), gap in zip(todo, gaps):
            back = jnp.dot(pair(gap), buf[s * ranks + r], preferred_element_type=F32)
            row = jnp.sum(back, axis=0, keepdims=True)
            for part in range(parts):
                out_ref[s, part, pl.ds(r, 1), :] = row
        return carry

    lax.fori_loop(0, lon // together, step, 0)


def spread(code_ref, adj_ref, buf, table, g, k, members, scaling):
    scale = (code_ref[g, k] >= 0).astype(F32) * scaling
    return buf.astype(F32) * (adj_ref[g, pl.ds(k, 1), :] * scale)


def ends_kernel(nb, blk, scaling, code_ref, adj_ref, table_ref, ens_ref, low_ref, high_ref, buf, sem):
    groups = code_ref.shape[0]
    low_ref[...] = jnp.zeros_like(low_ref)
    high_ref[...] = jnp.zeros_like(high_ref)

    def step(g, carry):
        for k in range(GROUP):
            code = code_ref[g, k]
            block = jnp.maximum(code, 0) % nb

            @pl.when((code >= 0) & ((block == 0) | (block == nb - 1)))
            def _():
                column = pl.multiple_of(block * blk, blk)
                copy = pltpu.make_async_copy(
                    ens_ref.at[code // nb, :, pl.ds(column, blk)], buf, sem
                )
                copy.start()
                copy.wait()
                part = buf[...].astype(F32) * (adj_ref[g, pl.ds(k, 1), :] * scaling)
                high, low = split(part)
                both = jnp.dot(
                    jnp.concatenate([high, low], axis=1), table_ref[...], preferred_element_type=F32
                )
                total = both[:, : 3 * blk] + both[:, 3 * blk :]

                @pl.when(block == 0)
                def _():
                    low_ref[...] += total[:, :blk]

                @pl.when(block == nb - 1)
                def _():
                    high_ref[...] += total[:, 2 * blk :]

        return carry

    lax.fori_loop(0, groups, step, 0)


def grad_kernel(nb, blk, scaling, code_ref, adj_ref, table_ref, ctrl_ref, ens_ref, out_ref,
                ext, buf, sems, row_sems):
    groups = code_ref.shape[0]
    members, nodes = ctrl_ref.shape
    copies = row_copies(ctrl_ref, ext, row_sems, pl.ds(blk, nodes))
    tile_copies(code_ref, ens_ref, buf, sems, nb, blk, groups)
    for copy in copies:
        copy.start()
    ext[:, :blk] = jnp.zeros((members, blk), F32)
    ext[:, nodes + blk :] = jnp.zeros((members, blk), F32)
    for copy in copies:
        copy.wait()

    def step(g, carry):
        wait_group(buf, sems, g)
        pieces = []
        for k in range(GROUP):
            scale = (code_ref[g, k] >= 0).astype(F32) * scaling
            pieces.append(buf[g * GROUP + k].astype(F32) * (adj_ref[g, pl.ds(k, 1), :] * scale))
        high, low = split(jnp.concatenate(pieces, axis=0))
        both = jnp.dot(
            jnp.concatenate([high, low], axis=1), table_ref[...], preferred_element_type=F32
        )
        total = both[:, : 3 * blk] + both[:, 3 * blk :]
        for k in range(GROUP):
            column = pl.multiple_of((jnp.maximum(code_ref[g, k], 0) % nb) * blk, blk)
            ext[:, pl.ds(column, 3 * blk)] += total[k * members : (k + 1) * members]
        return carry

    lax.fori_loop(0, groups, step, 0)
    count = row_sems.shape[0]
    rows = members // count
    copies = [
        pltpu.make_async_copy(
            ext.at[pl.ds(i * rows, rows), pl.ds(blk, nodes)],
            out_ref.at[pl.ds(i * rows, rows), :],
            row_sems.at[i],
        )
        for i in range(count)
    ]
    for copy in copies:
        copy.start()
    for copy in copies:
        copy.wait()


def edge_kernel(blk, grad_ref, before_ref, after_ref, out_ref, first, last, sems):
    nodes = grad_ref.shape[1]
    reads = [
        pltpu.make_async_copy(grad_ref.at[:, pl.ds(0, blk)], first, sems.at[0]),
        pltpu.make_async_copy(grad_ref.at[:, pl.ds(nodes - blk, blk)], last, sems.at[1]),
    ]
    for copy in reads:
        copy.start()
    for copy in reads:
        copy.wait()
    first[...] += before_ref[...]
    last[...] += after_ref[...]
    writes = [
        pltpu.make_async_copy(first, out_ref.at[:, pl.ds(0, blk)], sems.at[0]),
        pltpu.make_async_copy(last, out_ref.at[:, pl.ds(nodes - blk, blk)], sems.at[1]),
    ]
    for copy in writes:
        copy.start()
    for copy in writes:
        copy.wait()


def local(ensemble, control, obs_tiles, innovation, obs_weight, obs_counts, node_blocks, obs_slots):
    lon, mem = lax.axis_size("lon"), lax.axis_size("mem")
    obs, blk = obs_tiles.shape[0], obs_tiles.shape[2]
    members, nodes = control.shape
    nb = nodes // blk
    ranks = CAP // mem
    scaling = 1.0 / math.sqrt(members * mem - 1)
    slots = lon * CAP
    up = [(i, (i + 1) % lon) for i in range(lon)]
    down = [(j, i) for i, j in up]
    forward, backward = tables(blk)
    ens = jnp.transpose(ensemble, (1, 0, 2))
    dma = pltpu.SemaphoreType.DMA

    before = lax.ppermute(control[:, nodes - blk :], "lon", up)
    after = lax.ppermute(control[:, :blk], "lon", down)
    code, which = pl.pallas_call(
        functools.partial(index_kernel, nb, ranks),
        out_shape=(jax.ShapeDtypeStruct((lon, 128), jnp.int32),) * 2,
        in_specs=[VMEM, VMEM],
        out_specs=(VMEM, VMEM),
        name="index",
    )(node_blocks.reshape(lon, obs), obs_slots.reshape(lon, obs))

    part = pl.pallas_call(
        functools.partial(fetch_kernel, nb, blk, scaling),
        out_shape=jax.ShapeDtypeStruct((lon, CAP, blk), F32),
        in_specs=[SMEM, VMEM, VMEM, VMEM, ANY, ANY],
        out_specs=VMEM,
        scratch_shapes=[
            pltpu.VMEM((members, nodes + 2 * blk), F32),
            pltpu.VMEM((slots, members, blk), BF16),
            dma((lon,)),
            dma((8,)),
        ],
        compiler_params=params(),
        name="fetch",
    )(code, before, after, jnp.asarray(forward), control, ens)

    got = lax.all_to_all(
        part.reshape(lon * mem, ranks, blk), ("lon", "mem"), split_axis=0, concat_axis=0, tiled=True
    )
    back = pl.pallas_call(
        observe_kernel,
        out_shape=jax.ShapeDtypeStruct((lon, mem, ranks, blk), F32),
        in_specs=[SMEM, SMEM, VMEM, VMEM, VMEM, ANY],
        out_specs=VMEM,
        scratch_shapes=[pltpu.VMEM((lon * ranks, blk, blk), BF16), dma((lon,))],
        compiler_params=params(),
        name="observe",
    )(which, obs_counts, got.reshape(lon, mem, ranks, blk), innovation, obs_weight, obs_tiles)
    adj = lax.all_to_all(
        back.reshape(lon * mem, ranks, blk), ("lon", "mem"), split_axis=0, concat_axis=0, tiled=True
    ).reshape(lon, CAP, blk)

    table = jnp.asarray(backward)
    low, high = pl.pallas_call(
        functools.partial(ends_kernel, nb, blk, scaling),
        out_shape=(jax.ShapeDtypeStruct((members, blk), F32),) * 2,
        in_specs=[SMEM, VMEM, VMEM, ANY],
        out_specs=(VMEM, VMEM),
        scratch_shapes=[pltpu.VMEM((members, blk), BF16), dma(())],
        compiler_params=params(),
        name="ends",
    )(code, adj, table, ens)
    before = lax.ppermute(high, "lon", up)
    after = lax.ppermute(low, "lon", down)
    grad = pl.pallas_call(
        functools.partial(grad_kernel, nb, blk, scaling),
        out_shape=jax.ShapeDtypeStruct((members, nodes), F32),
        in_specs=[SMEM, VMEM, VMEM, ANY, ANY],
        out_specs=ANY,
        scratch_shapes=[
            pltpu.VMEM((members, nodes + 2 * blk), F32),
            pltpu.VMEM((slots, members, blk), BF16),
            dma((lon,)),
            dma((8,)),
        ],
        compiler_params=params(),
        cost_estimate=pl.CostEstimate(
            flops=6 * slots * members * blk * blk * 3,
            bytes_accessed=8 * members * nodes,
            transcendentals=0,
        ),
        name="grad",
    )(code, adj, table, control, ens)
    return pl.pallas_call(
        functools.partial(edge_kernel, blk),
        out_shape=jax.ShapeDtypeStruct((members, nodes), F32),
        in_specs=[ANY, VMEM, VMEM],
        out_specs=ANY,
        scratch_shapes=[pltpu.VMEM((members, blk), F32)] * 2 + [dma((2,))],
        input_output_aliases={0: 0},
        name="edge",
    )(grad, before, after)


def solution(mesh):
    return jax.shard_map(
        local,
        mesh=mesh,
        in_specs=(
            P("mem", None, "lon"),
            P("mem", "lon"),
            P("lon", None, None),
            P("lon", None),
            P("lon", None),
            P("lon"),
            P(),
            P(),
        ),
        out_specs=P("mem", "lon"),
        check_vma=False,
    )
```

```python
import functools
import math

import jax
import jax.numpy as jnp
import numpy as np
from jax import lax
from jax.experimental import pallas as pl
from jax.experimental.pallas import tpu as pltpu
from jax.sharding import PartitionSpec as P

CAP = 8
GROUP = 8
WIDE = 16
ROWS = 16
MESH = pl.DeviceIdType.MESH
F32 = jnp.float32
BF16 = jnp.bfloat16
ANY = pl.BlockSpec(memory_space=pl.ANY)
VMEM = pl.BlockSpec(memory_space=pltpu.VMEM)
SMEM = pl.BlockSpec(memory_space=pltpu.SMEM)
LIMIT = 60 << 20


def params(**kw):
    return pltpu.CompilerParams(vmem_limit_bytes=LIMIT, **kw)


def tables(blk):
    lag = np.arange(blk)[:, None] - np.arange(blk)[None, :]
    every = np.arange(-blk, blk + 1)
    norm = np.sqrt(np.sum(np.exp(-((3.0 * every / blk) ** 2))))
    parts = []
    for shift in range(3):
        cells = lag + (shift - 1) * blk
        raw = np.where(np.abs(cells) <= blk, np.exp(-0.5 * (3.0 * cells / blk) ** 2), 0.0)
        parts.append(raw / norm)
    bf = jnp.bfloat16.dtype if hasattr(jnp.bfloat16, "dtype") else np.dtype(jnp.bfloat16)

    def halves(value):
        high = value.astype(np.float32).astype(bf)
        low = (value - high.astype(np.float64)).astype(np.float32).astype(bf)
        return high, low

    high, low = halves(np.concatenate(parts, axis=0))
    forward = np.concatenate(
        [
            np.concatenate([high, low], axis=1),
            np.concatenate([high, np.zeros_like(low)], axis=1),
        ],
        axis=0,
    )
    high, low = halves(np.concatenate(parts[::-1], axis=1))
    backward = np.concatenate(
        [
            np.concatenate([high, low], axis=1),
            np.concatenate([high, np.zeros_like(low)], axis=1),
        ],
        axis=0,
    )
    return forward, backward


def split(value):
    high = value.astype(BF16)
    return high, (value - high.astype(F32)).astype(BF16)


def prepare_kernel(nb, blk, ranks, nodes_ref, slots_ref, ctrl_ref, code_ref, obs_ref, before_ref,
                   after_ref, land, sends, recvs):
    lon, obs = nodes_ref.shape
    nodes = ctrl_ref.shape[1]
    my, mm = lax.axis_index("lon"), lax.axis_index("mem")
    right, left = lax.rem(my + 1, lon), lax.rem(my + lon - 1, lon)
    barrier = pltpu.get_barrier_semaphore()
    for peer in (left, right):
        pl.semaphore_signal(barrier, inc=1, device_id=(peer, mm), device_id_type=MESH)
    pl.semaphore_wait(barrier, 2)
    copies = [
        pltpu.make_async_remote_copy(
            src_ref=ctrl_ref.at[:, pl.ds(start, blk)],
            dst_ref=land.at[side],
            send_sem=sends.at[side],
            recv_sem=recvs.at[side],
            device_id=(peer, mm),
            device_id_type=MESH,
        )
        for side, (start, peer) in enumerate(((nodes - blk, right), (0, left)))
    ]
    for copy in copies:
        copy.start()
    index_tables(nb, ranks, my, mm, nodes_ref, slots_ref, code_ref, obs_ref)
    for copy in copies:
        copy.wait()
    before_ref[...] = land[0]
    after_ref[...] = land[1]


def exchange_kernel(src_ref, out_ref, land, sends, recvs):
    count = src_ref.shape[0]
    parts = lax.axis_size("mem")
    me = lax.axis_index("lon") * parts + lax.axis_index("mem")
    barrier = pltpu.get_barrier_semaphore()

    def greet(off, carry):
        peer = lax.rem(me + off, count)
        pl.semaphore_signal(
            barrier, inc=1, device_id=(peer // parts, lax.rem(peer, parts)), device_id_type=MESH
        )
        return carry

    lax.fori_loop(1, count, greet, 0)
    pl.semaphore_wait(barrier, count - 1)

    def copy(off, peer, slot):
        return pltpu.make_async_remote_copy(
            src_ref=src_ref.at[peer],
            dst_ref=land.at[slot],
            send_sem=sends.at[off],
            recv_sem=recvs.at[off],
            device_id=(peer // parts, lax.rem(peer, parts)),
            device_id_type=MESH,
        )

    def send(off, carry):
        copy(off, lax.rem(me + off, count), me).start()
        return carry

    lax.fori_loop(1, count, send, 0)
    out_ref[pl.ds(me, 1)] = src_ref[pl.ds(me, 1)]

    def finish(off, carry):
        peer = lax.rem(me + off, count)
        source = lax.rem(me + count - off, count)
        copy(off, peer, source).wait_recv()
        out_ref[pl.ds(source, 1)] = land[pl.ds(source, 1)]
        copy(off, peer, source).wait_send()
        return carry

    lax.fori_loop(1, count, finish, 0)


def exchange(value, number):
    count = value.shape[0]
    return pl.pallas_call(
        exchange_kernel,
        out_shape=jax.ShapeDtypeStruct(value.shape, value.dtype),
        in_specs=[VMEM],
        out_specs=VMEM,
        scratch_shapes=[
            pltpu.VMEM(value.shape, value.dtype),
            pltpu.SemaphoreType.DMA((count,)),
            pltpu.SemaphoreType.DMA((count,)),
        ],
        compiler_params=pltpu.CompilerParams(collective_id=number, has_side_effects=True),
        name=f"exchange{number}",
    )(value)


def index_tables(nb, ranks, my, mm, nodes_ref, slots_ref, code_ref, obs_ref):
    lon, obs = nodes_ref.shape
    tri = (
        lax.broadcasted_iota(jnp.int32, (obs, obs), 0)
        < lax.broadcasted_iota(jnp.int32, (obs, obs), 1)
    ).astype(F32).astype(BF16)
    lane = lax.broadcasted_iota(jnp.int32, (lon, 128), 1)

    def ranked(match):
        return jnp.dot(match.astype(F32).astype(BF16), tri, preferred_element_type=F32)

    local = nodes_ref[...] - my * nb
    match = (local >= 0) & (local < nb)
    rank = ranked(match)
    value = (slots_ref[...] * nb + local + 1).astype(F32)
    code = jnp.zeros((lon, 128), F32)
    for k in range(CAP):
        hit = match & (rank == float(k))
        code = jnp.where(lane == k, jnp.sum(jnp.where(hit, value, 0.0), axis=1, keepdims=True), code)
    code_ref[...] = code.astype(jnp.int32) - 1

    base = lax.broadcasted_iota(jnp.int32, (lon, obs), 0) * nb
    mine = nodes_ref[pl.ds(my, 1), :] - base
    match = (mine >= 0) & (mine < nb)
    rank = ranked(match) - (mm * ranks).astype(F32)
    value = (lax.broadcasted_iota(jnp.int32, (lon, obs), 1) + 1).astype(F32)
    which = jnp.zeros((lon, 128), F32)
    for r in range(ranks):
        hit = match & (rank == float(r))
        which = jnp.where(lane == r, jnp.sum(jnp.where(hit, value, 0.0), axis=1, keepdims=True), which)
    obs_ref[...] = which.astype(jnp.int32) - 1


def tile_copies(code_ref, ens_ref, buf, sems, nb, blk, groups):
    def start(g, carry):
        for k in range(GROUP):
            code = jnp.maximum(code_ref[g, k], 0)
            column = pl.multiple_of((code % nb) * blk, blk)
            pltpu.make_async_copy(
                ens_ref.at[code // nb, :, pl.ds(column, blk)], buf.at[g * GROUP + k], sems.at[g]
            ).start()
        return carry

    lax.fori_loop(0, groups, start, 0)


def wait_group(buf, sems, g):
    view = buf.at[pl.ds(g * GROUP, GROUP)]
    pltpu.make_async_copy(view, view, sems.at[g]).wait()


def fetch_kernel(nb, blk, scaling, code_ref, before_ref, after_ref, table_ref, ctrl_ref, ens_ref,
                 out_ref, ext, buf, sems, row_sems):
    groups = code_ref.shape[0]
    members, nodes = ctrl_ref.shape
    chunks = members // ROWS
    copies = [
        pltpu.make_async_copy(
            ctrl_ref.at[pl.ds(i * 8, 8), :], ext.at[pl.ds(i * 8, 8), pl.ds(blk, nodes)], row_sems.at[i]
        )
        for i in range(members // 8)
    ]
    for copy in copies[: ROWS // 8]:
        copy.start()
    tile_copies(code_ref, ens_ref, buf, sems, nb, blk, groups)
    for copy in copies[ROWS // 8 :]:
        copy.start()
    ext[:, :blk] = before_ref[...]
    ext[:, nodes + blk :] = after_ref[...]
    per = WIDE // GROUP
    for c in range(chunks):
        for copy in copies[c * ROWS // 8 : (c + 1) * ROWS // 8]:
            copy.wait()
        rows = slice(c * ROWS, (c + 1) * ROWS)

        def step(i, carry):
            spots = [(i * per + j, k) for j in range(per) for k in range(GROUP)]
            pieces, live = [], []
            for g, k in spots:
                code = code_ref[g, k]
                live.append((code >= 0).astype(F32) * scaling)
                column = pl.multiple_of((jnp.maximum(code, 0) % nb) * blk, blk)
                pieces.append(ext[rows, pl.ds(column, 3 * blk)])
            high, low = split(jnp.concatenate(pieces, axis=0))
            both = jnp.dot(
                jnp.concatenate([high, low], axis=1), table_ref[...], preferred_element_type=F32
            )
            weights = both[:, :blk] + both[:, blk:]
            if c == 0:
                for j in range(per):
                    wait_group(buf, sems, i * per + j)
            for n, (g, k) in enumerate(spots):
                part = weights[n * ROWS : (n + 1) * ROWS] * buf[g * GROUP + k, rows].astype(F32)
                total = jnp.sum(part, axis=0, keepdims=True) * live[n]
                if c == 0:
                    out_ref[g, pl.ds(k, 1), :] = total
                else:
                    out_ref[g, pl.ds(k, 1), :] += total
            return carry

        lax.fori_loop(0, groups // per, step, 0)


def pair(row):
    high, low = split(row)
    index = lax.broadcasted_iota(jnp.int32, (16, row.shape[1]), 0)
    both = jnp.where(index == 0, high.astype(F32), jnp.where(index == 1, low.astype(F32), 0.0))
    return both.astype(BF16)


def observe_kernel(which_ref, counts_ref, got_ref, innov_ref, weight_ref, tiles_ref, out_ref,
                   buf, sems):
    lon, parts, ranks, blk = got_ref.shape

    def start(s, carry):
        for r in range(ranks):
            o = jnp.maximum(which_ref[s, r], 0)
            pltpu.make_async_copy(tiles_ref.at[o], buf.at[s * ranks + r], sems.at[s]).start()
        return carry

    lax.fori_loop(0, lon, start, 0)
    lane = lax.broadcasted_iota(jnp.int32, (1, blk), 1)
    together = 2 if lon % 2 == 0 else 1

    def step(i, carry):
        todo = []
        for j in range(together):
            s = i * together + j
            view = buf.at[pl.ds(s * ranks, ranks)]
            pltpu.make_async_copy(view, view, sems.at[s]).wait()
            rows = got_ref[s, 0]
            for part in range(1, parts):
                rows = rows + got_ref[s, part]
            for r in range(ranks):
                todo.append((s, r, rows[r : r + 1]))
        seen = [
            lax.dot_general(
                pair(row), buf[s * ranks + r], (((1,), (1,)), ((), ())), preferred_element_type=F32
            )
            for s, r, row in todo
        ]
        gaps = []
        for (s, r, _), value in zip(todo, seen):
            index = which_ref[s, r]
            o = jnp.maximum(index, 0)
            count = jnp.where(index >= 0, counts_ref[o], 0)
            observed = jnp.sum(value, axis=0, keepdims=True)
            gap = weight_ref[pl.ds(o, 1), :] * (observed - innov_ref[pl.ds(o, 1), :])
            gaps.append(jnp.where(lane < count, gap, 0.0))
        for (s, r, _), gap in zip(todo, gaps):
            back = jnp.dot(pair(gap), buf[s * ranks + r], preferred_element_type=F32)
            row = jnp.sum(back, axis=0, keepdims=True)
            for part in range(parts):
                out_ref[s, part, pl.ds(r, 1), :] = row
        return carry

    lax.fori_loop(0, lon // together, step, 0)


def grad_kernel(nb, blk, scaling, code_ref, adj_ref, table_ref, ctrl_ref, ens_ref, out_ref,
                low_ref, high_ref, ext, buf, sems, row_sems, out_sems):
    groups = code_ref.shape[0]
    members, nodes = ctrl_ref.shape
    chunks = members // ROWS
    copies = [
        pltpu.make_async_copy(
            ctrl_ref.at[pl.ds(i * 8, 8), :], ext.at[pl.ds(i * 8, 8), pl.ds(blk, nodes)], row_sems.at[i]
        )
        for i in range(members // 8)
    ]
    for copy in copies[: ROWS // 8]:
        copy.start()
    tile_copies(code_ref, ens_ref, buf, sems, nb, blk, groups)
    for copy in copies[ROWS // 8 :]:
        copy.start()
    ext[:, :blk] = jnp.zeros((members, blk), F32)
    ext[:, nodes + blk :] = jnp.zeros((members, blk), F32)
    per = WIDE // GROUP
    writes = []
    for c in range(chunks):
        for copy in copies[c * ROWS // 8 : (c + 1) * ROWS // 8]:
            copy.wait()
        rows = slice(c * ROWS, (c + 1) * ROWS)

        def step(i, carry):
            if c == 0:
                for j in range(per):
                    wait_group(buf, sems, i * per + j)
            spots = [(i * per + j, k) for j in range(per) for k in range(GROUP)]
            pieces = []
            for g, k in spots:
                scale = (code_ref[g, k] >= 0).astype(F32) * scaling
                row = adj_ref[g, pl.ds(k, 1), :] * scale
                pieces.append(buf[g * GROUP + k, rows].astype(F32) * row)
            high, low = split(jnp.concatenate(pieces, axis=0))
            both = jnp.dot(
                jnp.concatenate([high, low], axis=1), table_ref[...], preferred_element_type=F32
            )
            total = both[:, : 3 * blk] + both[:, 3 * blk :]
            for n, (g, k) in enumerate(spots):
                column = pl.multiple_of((jnp.maximum(code_ref[g, k], 0) % nb) * blk, blk)
                ext[rows, pl.ds(column, 3 * blk)] += total[n * ROWS : (n + 1) * ROWS]
            return carry

        lax.fori_loop(0, groups // per, step, 0)
        for i in range(c * ROWS // 8, (c + 1) * ROWS // 8):
            write = pltpu.make_async_copy(
                ext.at[pl.ds(i * 8, 8), pl.ds(blk, nodes)],
                out_ref.at[pl.ds(i * 8, 8), :],
                out_sems.at[i],
            )
            write.start()
            writes.append(write)
    low_ref[...] = ext[:, :blk]
    high_ref[...] = ext[:, nodes + blk :]
    for write in writes:
        write.wait()


def edge_kernel(blk, grad_ref, before_ref, after_ref, out_ref, first, last, sems):
    nodes = grad_ref.shape[1]
    reads = [
        pltpu.make_async_copy(grad_ref.at[:, pl.ds(0, blk)], first, sems.at[0]),
        pltpu.make_async_copy(grad_ref.at[:, pl.ds(nodes - blk, blk)], last, sems.at[1]),
    ]
    for copy in reads:
        copy.start()
    for copy in reads:
        copy.wait()
    first[...] += before_ref[...]
    last[...] += after_ref[...]
    writes = [
        pltpu.make_async_copy(first, out_ref.at[:, pl.ds(0, blk)], sems.at[0]),
        pltpu.make_async_copy(last, out_ref.at[:, pl.ds(nodes - blk, blk)], sems.at[1]),
    ]
    for copy in writes:
        copy.start()
    for copy in writes:
        copy.wait()


def local(ensemble, control, obs_tiles, innovation, obs_weight, obs_counts, node_blocks, obs_slots):
    lon, mem = lax.axis_size("lon"), lax.axis_size("mem")
    obs, blk = obs_tiles.shape[0], obs_tiles.shape[2]
    members, nodes = control.shape
    nb = nodes // blk
    ranks = CAP // mem
    scaling = 1.0 / math.sqrt(members * mem - 1)
    slots = lon * CAP
    up = [(i, (i + 1) % lon) for i in range(lon)]
    down = [(j, i) for i, j in up]
    forward, backward = tables(blk)
    ens = jnp.transpose(ensemble, (1, 0, 2))
    dma = pltpu.SemaphoreType.DMA

    code, which, before, after = pl.pallas_call(
        functools.partial(prepare_kernel, nb, blk, ranks),
        out_shape=(jax.ShapeDtypeStruct((lon, 128), jnp.int32),) * 2
        + (jax.ShapeDtypeStruct((members, blk), F32),) * 2,
        in_specs=[VMEM, VMEM, ANY],
        out_specs=(VMEM,) * 4,
        scratch_shapes=[pltpu.VMEM((2, members, blk), F32), dma((2,)), dma((2,))],
        compiler_params=pltpu.CompilerParams(collective_id=2, has_side_effects=True),
        name="prepare",
    )(node_blocks.reshape(lon, obs), obs_slots.reshape(lon, obs), control)

    part = pl.pallas_call(
        functools.partial(fetch_kernel, nb, blk, scaling),
        out_shape=jax.ShapeDtypeStruct((lon, CAP, blk), F32),
        in_specs=[SMEM, VMEM, VMEM, VMEM, ANY, ANY],
        out_specs=VMEM,
        scratch_shapes=[
            pltpu.VMEM((members, nodes + 2 * blk), F32),
            pltpu.VMEM((slots, members, blk), BF16),
            dma((lon,)),
            dma((members // 8,)),
        ],
        compiler_params=params(),
        name="fetch",
    )(code, before, after, jnp.asarray(forward), control, ens)

    got = exchange(part.reshape(lon * mem, ranks, blk), 0)
    back = pl.pallas_call(
        observe_kernel,
        out_shape=jax.ShapeDtypeStruct((lon, mem, ranks, blk), F32),
        in_specs=[SMEM, SMEM, VMEM, VMEM, VMEM, ANY],
        out_specs=VMEM,
        scratch_shapes=[pltpu.VMEM((lon * ranks, blk, blk), BF16), dma((lon,))],
        compiler_params=params(),
        name="observe",
    )(which, obs_counts, got.reshape(lon, mem, ranks, blk), innovation, obs_weight, obs_tiles)
    adj = exchange(back.reshape(lon * mem, ranks, blk), 1).reshape(lon, CAP, blk)

    table = jnp.asarray(backward)
    grad, low, high = pl.pallas_call(
        functools.partial(grad_kernel, nb, blk, scaling),
        out_shape=(jax.ShapeDtypeStruct((members, nodes), F32),)
        + (jax.ShapeDtypeStruct((members, blk), F32),) * 2,
        in_specs=[SMEM, VMEM, VMEM, ANY, ANY],
        out_specs=(ANY, VMEM, VMEM),
        scratch_shapes=[
            pltpu.VMEM((members, nodes + 2 * blk), F32),
            pltpu.VMEM((slots, members, blk), BF16),
            dma((lon,)),
            dma((members // 8,)),
            dma((members // 8,)),
        ],
        compiler_params=params(),
        name="grad",
    )(code, adj, table, control, ens)
    before = lax.ppermute(high, "lon", up)
    after = lax.ppermute(low, "lon", down)
    return pl.pallas_call(
        functools.partial(edge_kernel, blk),
        out_shape=jax.ShapeDtypeStruct((members, nodes), F32),
        in_specs=[ANY, VMEM, VMEM],
        out_specs=ANY,
        scratch_shapes=[pltpu.VMEM((members, blk), F32)] * 2 + [dma((2,))],
        input_output_aliases={0: 0},
        name="edge",
    )(grad, before, after)


def solution(mesh):
    return jax.shard_map(
        local,
        mesh=mesh,
        in_specs=(
            P("mem", None, "lon"),
            P("mem", "lon"),
            P("lon", None, None),
            P("lon", None),
            P("lon", None),
            P("lon"),
            P(),
            P(),
        ),
        out_specs=P("mem", "lon"),
        check_vma=False,
    )
```

```python
import functools
import math

import jax
import jax.numpy as jnp
import numpy as np
from jax import lax
from jax.experimental import pallas as pl
from jax.experimental.pallas import tpu as pltpu
from jax.sharding import PartitionSpec as P

CAP = 8
GROUP = 8
WIDE = 16
ROWS = 16
MESH = pl.DeviceIdType.MESH
F32 = jnp.float32
BF16 = jnp.bfloat16
ANY = pl.BlockSpec(memory_space=pl.ANY)
VMEM = pl.BlockSpec(memory_space=pltpu.VMEM)
SMEM = pl.BlockSpec(memory_space=pltpu.SMEM)
LIMIT = 60 << 20


def params(**kw):
    return pltpu.CompilerParams(vmem_limit_bytes=LIMIT, **kw)


def tables(blk):
    lag = np.arange(blk)[:, None] - np.arange(blk)[None, :]
    every = np.arange(-blk, blk + 1)
    norm = np.sqrt(np.sum(np.exp(-((3.0 * every / blk) ** 2))))
    parts = []
    for shift in range(3):
        cells = lag + (shift - 1) * blk
        raw = np.where(np.abs(cells) <= blk, np.exp(-0.5 * (3.0 * cells / blk) ** 2), 0.0)
        parts.append(raw / norm)
    bf = jnp.bfloat16.dtype if hasattr(jnp.bfloat16, "dtype") else np.dtype(jnp.bfloat16)

    def halves(value):
        high = value.astype(np.float32).astype(bf)
        low = (value - high.astype(np.float64)).astype(np.float32).astype(bf)
        return high, low

    high, low = halves(np.concatenate(parts, axis=0))
    forward = np.concatenate(
        [
            np.concatenate([high, low], axis=1),
            np.concatenate([high, np.zeros_like(low)], axis=1),
        ],
        axis=0,
    )
    high, low = halves(np.concatenate(parts[::-1], axis=1))
    backward = np.concatenate(
        [
            np.concatenate([high, low], axis=1),
            np.concatenate([high, np.zeros_like(low)], axis=1),
        ],
        axis=0,
    )
    return forward, backward


def split(value):
    high = value.astype(BF16)
    return high, (value - high.astype(F32)).astype(BF16)


def prepare_kernel(nb, blk, ranks, nodes_ref, slots_ref, ctrl_ref, code_ref, slot_ref, obs_ref,
                   before_ref, after_ref, land, sends, recvs):
    lon, obs = nodes_ref.shape
    nodes = ctrl_ref.shape[1]
    my, mm = lax.axis_index("lon"), lax.axis_index("mem")
    right, left = lax.rem(my + 1, lon), lax.rem(my + lon - 1, lon)
    barrier = pltpu.get_barrier_semaphore()
    for peer in (left, right):
        pl.semaphore_signal(barrier, inc=1, device_id=(peer, mm), device_id_type=MESH)
    pl.semaphore_wait(barrier, 2)
    copies = [
        pltpu.make_async_remote_copy(
            src_ref=ctrl_ref.at[:, pl.ds(start, blk)],
            dst_ref=land.at[side],
            send_sem=sends.at[side],
            recv_sem=recvs.at[side],
            device_id=(peer, mm),
            device_id_type=MESH,
        )
        for side, (start, peer) in enumerate(((nodes - blk, right), (0, left)))
    ]
    for copy in copies:
        copy.start()
    index_tables(nb, blk, ranks, my, mm, nodes_ref, slots_ref, code_ref, slot_ref, obs_ref)
    for copy in copies:
        copy.wait()
    before_ref[...] = land[0]
    after_ref[...] = land[1]


def exchange_kernel(src_ref, out_ref, land, sends, recvs):
    lon, mem = lax.axis_size("lon"), lax.axis_size("mem")
    me = lax.axis_index("lon") * mem + lax.axis_index("mem")
    barrier = pltpu.get_barrier_semaphore()

    def others(act):
        def step(a, carry):
            for b in range(mem):
                pl.when(a * mem + b != me)(functools.partial(act, a, b, a * mem + b))
            return carry

        lax.fori_loop(0, lon, step, 0)

    def greet(a, b, peer):
        pl.semaphore_signal(barrier, inc=1, device_id=(a, b), device_id_type=MESH)

    def copy(a, b, peer, slot):
        return pltpu.make_async_remote_copy(
            src_ref=src_ref.at[peer],
            dst_ref=land.at[slot],
            send_sem=sends.at[peer],
            recv_sem=recvs.at[slot],
            device_id=(a, b),
            device_id_type=MESH,
        )

    def send(a, b, peer):
        copy(a, b, peer, me).start()

    def finish(a, b, peer):
        copy(a, b, peer, peer).wait_recv()
        copy(a, b, peer, peer).wait_send()

    others(greet)
    land[pl.ds(me, 1)] = src_ref[pl.ds(me, 1)]
    pl.semaphore_wait(barrier, lon * mem - 1)
    others(send)
    others(finish)
    out_ref[...] = land[...]


def exchange(value, number):
    count = value.shape[0]
    return pl.pallas_call(
        exchange_kernel,
        out_shape=jax.ShapeDtypeStruct(value.shape, value.dtype),
        in_specs=[VMEM],
        out_specs=VMEM,
        scratch_shapes=[
            pltpu.VMEM(value.shape, value.dtype),
            pltpu.SemaphoreType.DMA((count,)),
            pltpu.SemaphoreType.DMA((count,)),
        ],
        compiler_params=pltpu.CompilerParams(collective_id=number, has_side_effects=True),
        name=f"exchange{number}",
    )(value)


def index_tables(nb, blk, ranks, my, mm, nodes_ref, slots_ref, code_ref, slot_ref, obs_ref):
    lon, obs = nodes_ref.shape
    tri = (
        lax.broadcasted_iota(jnp.int32, (obs, obs), 0)
        < lax.broadcasted_iota(jnp.int32, (obs, obs), 1)
    ).astype(F32).astype(BF16)
    lane = lax.broadcasted_iota(jnp.int32, (lon, 128), 1)

    def ranked(match):
        return jnp.dot(match.astype(F32).astype(BF16), tri, preferred_element_type=F32)

    local = nodes_ref[...] - my * nb
    match = (local >= 0) & (local < nb)
    rank = ranked(match)
    column = (local * blk).astype(F32)
    slot = slots_ref[...].astype(F32)
    columns = jnp.zeros((lon, 128), F32)
    slots = jnp.zeros((lon, 128), F32)
    for k in range(CAP):
        hit = match & (rank == float(k))
        columns = jnp.where(
            lane == k, jnp.sum(jnp.where(hit, column, 0.0), axis=1, keepdims=True), columns
        )
        slots = jnp.where(
            lane == k, jnp.sum(jnp.where(hit, slot, 0.0), axis=1, keepdims=True), slots
        )
    code_ref[...] = columns.astype(jnp.int32)
    slot_ref[...] = slots.astype(jnp.int32)

    base = lax.broadcasted_iota(jnp.int32, (lon, obs), 0) * nb
    mine = nodes_ref[pl.ds(my, 1), :] - base
    match = (mine >= 0) & (mine < nb)
    rank = ranked(match) - (mm * ranks).astype(F32)
    value = (lax.broadcasted_iota(jnp.int32, (lon, obs), 1) + 1).astype(F32)
    which = jnp.zeros((lon, 128), F32)
    for r in range(ranks):
        hit = match & (rank == float(r))
        which = jnp.where(lane == r, jnp.sum(jnp.where(hit, value, 0.0), axis=1, keepdims=True), which)
    obs_ref[...] = which.astype(jnp.int32) - 1


def tile_copies(code_ref, slot_ref, ens_ref, buf, sems, blk, groups):
    def start(g, carry):
        for k in range(GROUP):
            column = pl.multiple_of(code_ref[g, k], blk)
            pltpu.make_async_copy(
                ens_ref.at[slot_ref[g, k], :, pl.ds(column, blk)], buf.at[g * GROUP + k], sems.at[g]
            ).start()
        return carry

    lax.fori_loop(0, groups, start, 0)


def wait_group(buf, sems, g):
    view = buf.at[pl.ds(g * GROUP, GROUP)]
    pltpu.make_async_copy(view, view, sems.at[g]).wait()


def fetch_kernel(blk, scaling, code_ref, slot_ref, before_ref, after_ref, table_ref, ctrl_ref, ens_ref,
                 out_ref, ext, buf, sems, row_sems):
    groups = code_ref.shape[0]
    members, nodes = ctrl_ref.shape
    chunks = members // ROWS
    copies = [
        pltpu.make_async_copy(
            ctrl_ref.at[pl.ds(i * 8, 8), :], ext.at[pl.ds(i * 8, 8), pl.ds(blk, nodes)], row_sems.at[i]
        )
        for i in range(members // 8)
    ]
    for copy in copies[: ROWS // 8]:
        copy.start()
    tile_copies(code_ref, slot_ref, ens_ref, buf, sems, blk, groups)
    for copy in copies[ROWS // 8 :]:
        copy.start()
    ext[:, :blk] = before_ref[...]
    ext[:, nodes + blk :] = after_ref[...]
    per = WIDE // GROUP
    for c in range(chunks):
        for copy in copies[c * ROWS // 8 : (c + 1) * ROWS // 8]:
            copy.wait()
        rows = slice(c * ROWS, (c + 1) * ROWS)

        def step(i, carry):
            spots = [(i * per + j, k) for j in range(per) for k in range(GROUP)]
            pieces = []
            for g, k in spots:
                column = pl.multiple_of(code_ref[g, k], blk)
                pieces.append(ext[rows, pl.ds(column, 3 * blk)])
            high, low = split(jnp.concatenate(pieces, axis=0))
            both = jnp.dot(
                jnp.concatenate([high, low], axis=1), table_ref[...], preferred_element_type=F32
            )
            weights = both[:, :blk] + both[:, blk:]
            if c == 0:
                for j in range(per):
                    wait_group(buf, sems, i * per + j)
            for n, (g, k) in enumerate(spots):
                part = weights[n * ROWS : (n + 1) * ROWS] * buf[g * GROUP + k, rows].astype(F32)
                total = jnp.sum(part, axis=0, keepdims=True) * scaling
                if c == 0:
                    out_ref[g, pl.ds(k, 1), :] = total
                else:
                    out_ref[g, pl.ds(k, 1), :] += total
            return carry

        lax.fori_loop(0, groups // per, step, 0)


def pair(row):
    high, low = split(row)
    index = lax.broadcasted_iota(jnp.int32, (16, row.shape[1]), 0)
    both = jnp.where(index == 0, high.astype(F32), jnp.where(index == 1, low.astype(F32), 0.0))
    return both.astype(BF16)


def observe_kernel(which_ref, counts_ref, got_ref, innov_ref, weight_ref, tiles_ref, out_ref,
                   buf, sems):
    lon, parts, ranks, blk = got_ref.shape

    def start(s, carry):
        for r in range(ranks):
            o = jnp.maximum(which_ref[s, r], 0)
            pltpu.make_async_copy(tiles_ref.at[o], buf.at[s * ranks + r], sems.at[s]).start()
        return carry

    lax.fori_loop(0, lon, start, 0)
    lane = lax.broadcasted_iota(jnp.int32, (1, blk), 1)
    together = 2 if lon % 2 == 0 else 1

    def step(i, carry):
        todo = []
        for j in range(together):
            s = i * together + j
            view = buf.at[pl.ds(s * ranks, ranks)]
            pltpu.make_async_copy(view, view, sems.at[s]).wait()
            rows = got_ref[s, 0]
            for part in range(1, parts):
                rows = rows + got_ref[s, part]
            for r in range(ranks):
                todo.append((s, r, rows[r : r + 1]))
        seen = [
            lax.dot_general(
                pair(row), buf[s * ranks + r], (((1,), (1,)), ((), ())), preferred_element_type=F32
            )
            for s, r, row in todo
        ]
        gaps = []
        for (s, r, _), value in zip(todo, seen):
            index = which_ref[s, r]
            o = jnp.maximum(index, 0)
            count = jnp.where(index >= 0, counts_ref[o], 0)
            observed = jnp.sum(value, axis=0, keepdims=True)
            gap = weight_ref[pl.ds(o, 1), :] * (observed - innov_ref[pl.ds(o, 1), :])
            gaps.append(jnp.where(lane < count, gap, 0.0))
        for (s, r, _), gap in zip(todo, gaps):
            back = jnp.dot(pair(gap), buf[s * ranks + r], preferred_element_type=F32)
            row = jnp.sum(back, axis=0, keepdims=True)
            for part in range(parts):
                out_ref[s, part, pl.ds(r, 1), :] = row
        return carry

    lax.fori_loop(0, lon // together, step, 0)


def grad_kernel(blk, scaling, code_ref, slot_ref, adj_ref, table_ref, ctrl_ref, ens_ref, out_ref,
                low_ref, high_ref, ext, buf, sems, row_sems, out_sems):
    groups = code_ref.shape[0]
    members, nodes = ctrl_ref.shape
    chunks = members // ROWS
    copies = [
        pltpu.make_async_copy(
            ctrl_ref.at[pl.ds(i * 8, 8), :], ext.at[pl.ds(i * 8, 8), pl.ds(blk, nodes)], row_sems.at[i]
        )
        for i in range(members // 8)
    ]
    for copy in copies[: ROWS // 8]:
        copy.start()
    tile_copies(code_ref, slot_ref, ens_ref, buf, sems, blk, groups)
    for copy in copies[ROWS // 8 :]:
        copy.start()
    ext[:, :blk] = jnp.zeros((members, blk), F32)
    ext[:, nodes + blk :] = jnp.zeros((members, blk), F32)
    per = WIDE // GROUP
    writes = []
    for c in range(chunks):
        for copy in copies[c * ROWS // 8 : (c + 1) * ROWS // 8]:
            copy.wait()
        rows = slice(c * ROWS, (c + 1) * ROWS)

        def step(i, carry):
            if c == 0:
                for j in range(per):
                    wait_group(buf, sems, i * per + j)
            spots = [(i * per + j, k) for j in range(per) for k in range(GROUP)]
            pieces = []
            for g, k in spots:
                row = adj_ref[g, pl.ds(k, 1), :] * scaling
                pieces.append(buf[g * GROUP + k, rows].astype(F32) * row)
            high, low = split(jnp.concatenate(pieces, axis=0))
            both = jnp.dot(
                jnp.concatenate([high, low], axis=1), table_ref[...], preferred_element_type=F32
            )
            total = both[:, : 3 * blk] + both[:, 3 * blk :]
            for n, (g, k) in enumerate(spots):
                column = pl.multiple_of(code_ref[g, k], blk)
                ext[rows, pl.ds(column, 3 * blk)] += total[n * ROWS : (n + 1) * ROWS]
            return carry

        lax.fori_loop(0, groups // per, step, 0)
        for i in range(c * ROWS // 8, (c + 1) * ROWS // 8):
            write = pltpu.make_async_copy(
                ext.at[pl.ds(i * 8, 8), pl.ds(blk, nodes)],
                out_ref.at[pl.ds(i * 8, 8), :],
                out_sems.at[i],
            )
            write.start()
            writes.append(write)
    low_ref[...] = ext[:, :blk]
    high_ref[...] = ext[:, nodes + blk :]
    for write in writes:
        write.wait()


def edge_kernel(blk, grad_ref, before_ref, after_ref, out_ref, first, last, sems):
    nodes = grad_ref.shape[1]
    reads = [
        pltpu.make_async_copy(grad_ref.at[:, pl.ds(0, blk)], first, sems.at[0]),
        pltpu.make_async_copy(grad_ref.at[:, pl.ds(nodes - blk, blk)], last, sems.at[1]),
    ]
    for copy in reads:
        copy.start()
    for copy in reads:
        copy.wait()
    first[...] += before_ref[...]
    last[...] += after_ref[...]
    writes = [
        pltpu.make_async_copy(first, out_ref.at[:, pl.ds(0, blk)], sems.at[0]),
        pltpu.make_async_copy(last, out_ref.at[:, pl.ds(nodes - blk, blk)], sems.at[1]),
    ]
    for copy in writes:
        copy.start()
    for copy in writes:
        copy.wait()


def local(ensemble, control, obs_tiles, innovation, obs_weight, obs_counts, node_blocks, obs_slots):
    lon, mem = lax.axis_size("lon"), lax.axis_size("mem")
    obs, blk = obs_tiles.shape[0], obs_tiles.shape[2]
    members, nodes = control.shape
    nb = nodes // blk
    ranks = CAP // mem
    scaling = 1.0 / math.sqrt(members * mem - 1)
    slots = lon * CAP
    up = [(i, (i + 1) % lon) for i in range(lon)]
    down = [(j, i) for i, j in up]
    forward, backward = tables(blk)
    ens = jnp.transpose(ensemble, (1, 0, 2))
    dma = pltpu.SemaphoreType.DMA

    code, slot, which, before, after = pl.pallas_call(
        functools.partial(prepare_kernel, nb, blk, ranks),
        out_shape=(jax.ShapeDtypeStruct((lon, 128), jnp.int32),) * 3
        + (jax.ShapeDtypeStruct((members, blk), F32),) * 2,
        in_specs=[VMEM, VMEM, ANY],
        out_specs=(VMEM,) * 5,
        scratch_shapes=[pltpu.VMEM((2, members, blk), F32), dma((2,)), dma((2,))],
        compiler_params=pltpu.CompilerParams(collective_id=2, has_side_effects=True),
        name="prepare",
    )(node_blocks.reshape(lon, obs), obs_slots.reshape(lon, obs), control)

    part = pl.pallas_call(
        functools.partial(fetch_kernel, blk, scaling),
        out_shape=jax.ShapeDtypeStruct((lon, CAP, blk), F32),
        in_specs=[SMEM, SMEM, VMEM, VMEM, VMEM, ANY, ANY],
        out_specs=VMEM,
        scratch_shapes=[
            pltpu.VMEM((members, nodes + 2 * blk), F32),
            pltpu.VMEM((slots, members, blk), BF16),
            dma((lon,)),
            dma((members // 8,)),
        ],
        compiler_params=params(),
        name="fetch",
    )(code, slot, before, after, jnp.asarray(forward), control, ens)

    got = exchange(part.reshape(lon * mem, ranks, blk), 0)
    back = pl.pallas_call(
        observe_kernel,
        out_shape=jax.ShapeDtypeStruct((lon, mem, ranks, blk), F32),
        in_specs=[SMEM, SMEM, VMEM, VMEM, VMEM, ANY],
        out_specs=VMEM,
        scratch_shapes=[pltpu.VMEM((lon * ranks, blk, blk), BF16), dma((lon,))],
        compiler_params=params(),
        name="observe",
    )(which, obs_counts, got.reshape(lon, mem, ranks, blk), innovation, obs_weight, obs_tiles)
    adj = exchange(back.reshape(lon * mem, ranks, blk), 1).reshape(lon, CAP, blk)

    table = jnp.asarray(backward)
    grad, low, high = pl.pallas_call(
        functools.partial(grad_kernel, blk, scaling),
        out_shape=(jax.ShapeDtypeStruct((members, nodes), F32),)
        + (jax.ShapeDtypeStruct((members, blk), F32),) * 2,
        in_specs=[SMEM, SMEM, VMEM, VMEM, ANY, ANY],
        out_specs=(ANY, VMEM, VMEM),
        scratch_shapes=[
            pltpu.VMEM((members, nodes + 2 * blk), F32),
            pltpu.VMEM((slots, members, blk), BF16),
            dma((lon,)),
            dma((members // 8,)),
            dma((members // 8,)),
        ],
        compiler_params=params(),
        name="grad",
    )(code, slot, adj, table, control, ens)
    before = lax.ppermute(high, "lon", up)
    after = lax.ppermute(low, "lon", down)
    return pl.pallas_call(
        functools.partial(edge_kernel, blk),
        out_shape=jax.ShapeDtypeStruct((members, nodes), F32),
        in_specs=[ANY, VMEM, VMEM],
        out_specs=ANY,
        scratch_shapes=[pltpu.VMEM((members, blk), F32)] * 2 + [dma((2,))],
        input_output_aliases={0: 0},
        name="edge",
    )(grad, before, after)


def solution(mesh):
    return jax.shard_map(
        local,
        mesh=mesh,
        in_specs=(
            P("mem", None, "lon"),
            P("mem", "lon"),
            P("lon", None, None),
            P("lon", None),
            P("lon", None),
            P("lon"),
            P(),
            P(),
        ),
        out_specs=P("mem", "lon"),
        check_vma=False,
    )
```

```python
import functools
import math

import jax
import jax.numpy as jnp
import numpy as np
from jax import lax
from jax.experimental import pallas as pl
from jax.experimental.pallas import tpu as pltpu
from jax.sharding import PartitionSpec as P

CAP = 8
GROUP = 8
WIDE = 32
WIDE_FETCH = 64
ROWS = 16
MESH = pl.DeviceIdType.MESH
F32 = jnp.float32
BF16 = jnp.bfloat16
ANY = pl.BlockSpec(memory_space=pl.ANY)
VMEM = pl.BlockSpec(memory_space=pltpu.VMEM)
SMEM = pl.BlockSpec(memory_space=pltpu.SMEM)
LIMIT = 60 << 20


def params(**kw):
    return pltpu.CompilerParams(vmem_limit_bytes=LIMIT, **kw)


def tables(blk):
    lag = np.arange(blk)[:, None] - np.arange(blk)[None, :]
    every = np.arange(-blk, blk + 1)
    norm = np.sqrt(np.sum(np.exp(-((3.0 * every / blk) ** 2))))
    parts = []
    for shift in range(3):
        cells = lag + (shift - 1) * blk
        raw = np.where(np.abs(cells) <= blk, np.exp(-0.5 * (3.0 * cells / blk) ** 2), 0.0)
        parts.append(raw / norm)
    bf = jnp.bfloat16.dtype if hasattr(jnp.bfloat16, "dtype") else np.dtype(jnp.bfloat16)

    def halves(value):
        high = value.astype(np.float32).astype(bf)
        low = (value - high.astype(np.float64)).astype(np.float32).astype(bf)
        return high, low

    high, low = halves(np.concatenate(parts, axis=0))
    forward = np.concatenate(
        [
            np.concatenate([high, low], axis=1),
            np.concatenate([high, np.zeros_like(low)], axis=1),
        ],
        axis=0,
    )
    high, low = halves(np.concatenate(parts[::-1], axis=1))
    backward = np.concatenate(
        [
            np.concatenate([high, low], axis=1),
            np.concatenate([high, np.zeros_like(low)], axis=1),
        ],
        axis=0,
    )
    return forward, backward


def split(value):
    high = value.astype(BF16)
    return high, (value - high.astype(F32)).astype(BF16)


def prepare_kernel(nb, blk, ranks, nodes_ref, slots_ref, ctrl_ref, code_ref, slot_ref, obs_ref,
                   before_ref, after_ref, land, sends, recvs):
    lon, obs = nodes_ref.shape
    nodes = ctrl_ref.shape[1]
    my, mm = lax.axis_index("lon"), lax.axis_index("mem")
    right, left = lax.rem(my + 1, lon), lax.rem(my + lon - 1, lon)
    barrier = pltpu.get_barrier_semaphore()
    for peer in (left, right):
        pl.semaphore_signal(barrier, inc=1, device_id=(peer, mm), device_id_type=MESH)
    pl.semaphore_wait(barrier, 2)
    copies = [
        pltpu.make_async_remote_copy(
            src_ref=ctrl_ref.at[:, pl.ds(start, blk)],
            dst_ref=land.at[side],
            send_sem=sends.at[side],
            recv_sem=recvs.at[side],
            device_id=(peer, mm),
            device_id_type=MESH,
        )
        for side, (start, peer) in enumerate(((nodes - blk, right), (0, left)))
    ]
    for copy in copies:
        copy.start()
    index_tables(nb, blk, ranks, my, mm, nodes_ref, slots_ref, code_ref, slot_ref, obs_ref)
    for copy in copies:
        copy.wait()
    before_ref[...] = land[0]
    after_ref[...] = land[1]


def exchange_kernel(src_ref, out_ref, land, sends, recvs):
    lon, mem = lax.axis_size("lon"), lax.axis_size("mem")
    me = lax.axis_index("lon") * mem + lax.axis_index("mem")
    barrier = pltpu.get_barrier_semaphore()

    def others(act):
        def step(a, carry):
            for b in range(mem):
                pl.when(a * mem + b != me)(functools.partial(act, a, b, a * mem + b))
            return carry

        lax.fori_loop(0, lon, step, 0)

    def greet(a, b, peer):
        pl.semaphore_signal(barrier, inc=1, device_id=(a, b), device_id_type=MESH)

    def copy(a, b, peer, slot):
        return pltpu.make_async_remote_copy(
            src_ref=src_ref.at[peer],
            dst_ref=land.at[slot],
            send_sem=sends.at[peer],
            recv_sem=recvs.at[slot],
            device_id=(a, b),
            device_id_type=MESH,
        )

    def send(a, b, peer):
        copy(a, b, peer, me).start()

    def finish(a, b, peer):
        copy(a, b, peer, peer).wait_recv()
        copy(a, b, peer, peer).wait_send()

    others(greet)
    land[pl.ds(me, 1)] = src_ref[pl.ds(me, 1)]
    pl.semaphore_wait(barrier, lon * mem - 1)
    others(send)
    others(finish)
    out_ref[...] = land[...]


def exchange(value, number):
    count = value.shape[0]
    return pl.pallas_call(
        exchange_kernel,
        out_shape=jax.ShapeDtypeStruct(value.shape, value.dtype),
        in_specs=[VMEM],
        out_specs=VMEM,
        scratch_shapes=[
            pltpu.VMEM(value.shape, value.dtype),
            pltpu.SemaphoreType.DMA((count,)),
            pltpu.SemaphoreType.DMA((count,)),
        ],
        compiler_params=pltpu.CompilerParams(collective_id=number, has_side_effects=True),
        name=f"exchange{number}",
    )(value)


def index_tables(nb, blk, ranks, my, mm, nodes_ref, slots_ref, code_ref, slot_ref, obs_ref):
    lon, obs = nodes_ref.shape
    tri = (
        lax.broadcasted_iota(jnp.int32, (obs, obs), 0)
        < lax.broadcasted_iota(jnp.int32, (obs, obs), 1)
    ).astype(F32).astype(BF16)
    lane = lax.broadcasted_iota(jnp.int32, (lon, 128), 1)

    def ranked(match):
        return jnp.dot(match.astype(F32).astype(BF16), tri, preferred_element_type=F32)

    local = nodes_ref[...] - my * nb
    match = (local >= 0) & (local < nb)
    rank = ranked(match)
    column = (local * blk).astype(F32)
    slot = slots_ref[...].astype(F32)
    columns = jnp.zeros((lon, 128), F32)
    slots = jnp.zeros((lon, 128), F32)
    for k in range(CAP):
        hit = match & (rank == float(k))
        columns = jnp.where(
            lane == k, jnp.sum(jnp.where(hit, column, 0.0), axis=1, keepdims=True), columns
        )
        slots = jnp.where(
            lane == k, jnp.sum(jnp.where(hit, slot, 0.0), axis=1, keepdims=True), slots
        )
    code_ref[...] = columns.astype(jnp.int32)
    slot_ref[...] = slots.astype(jnp.int32)

    base = lax.broadcasted_iota(jnp.int32, (lon, obs), 0) * nb
    mine = nodes_ref[pl.ds(my, 1), :] - base
    match = (mine >= 0) & (mine < nb)
    rank = ranked(match) - (mm * ranks).astype(F32)
    value = (lax.broadcasted_iota(jnp.int32, (lon, obs), 1) + 1).astype(F32)
    which = jnp.zeros((lon, 128), F32)
    for r in range(ranks):
        hit = match & (rank == float(r))
        which = jnp.where(lane == r, jnp.sum(jnp.where(hit, value, 0.0), axis=1, keepdims=True), which)
    obs_ref[...] = which.astype(jnp.int32) - 1


def tile_copies(code_ref, slot_ref, ens_ref, buf, sems, blk, groups):
    def start(g, carry):
        for k in range(GROUP):
            column = pl.multiple_of(code_ref[g, k], blk)
            pltpu.make_async_copy(
                ens_ref.at[slot_ref[g, k], :, pl.ds(column, blk)], buf.at[g * GROUP + k], sems.at[g]
            ).start()
        return carry

    lax.fori_loop(0, groups, start, 0)


def wait_group(buf, sems, g):
    view = buf.at[pl.ds(g * GROUP, GROUP)]
    pltpu.make_async_copy(view, view, sems.at[g]).wait()


def fetch_kernel(blk, scaling, code_ref, slot_ref, before_ref, after_ref, table_ref, ctrl_ref, ens_ref,
                 out_ref, ext, buf, sems, row_sems):
    groups = code_ref.shape[0]
    members, nodes = ctrl_ref.shape
    chunks = members // ROWS
    copies = [
        pltpu.make_async_copy(
            ctrl_ref.at[pl.ds(i * 8, 8), :], ext.at[pl.ds(i * 8, 8), pl.ds(blk, nodes)], row_sems.at[i]
        )
        for i in range(members // 8)
    ]
    for copy in copies[: ROWS // 8]:
        copy.start()
    tile_copies(code_ref, slot_ref, ens_ref, buf, sems, blk, groups)
    for copy in copies[ROWS // 8 :]:
        copy.start()
    ext[:, :blk] = before_ref[...]
    ext[:, nodes + blk :] = after_ref[...]
    per = WIDE_FETCH // GROUP
    for c in range(chunks):
        for copy in copies[c * ROWS // 8 : (c + 1) * ROWS // 8]:
            copy.wait()
        rows = slice(c * ROWS, (c + 1) * ROWS)

        def step(i, carry):
            spots = [(i * per + j, k) for j in range(per) for k in range(GROUP)]
            pieces = []
            for g, k in spots:
                column = pl.multiple_of(code_ref[g, k], blk)
                pieces.append(ext[rows, pl.ds(column, 3 * blk)])
            high, low = split(jnp.concatenate(pieces, axis=0))
            both = jnp.dot(
                jnp.concatenate([high, low], axis=1), table_ref[...], preferred_element_type=F32
            )
            weights = both[:, :blk] + both[:, blk:]
            if c == 0:
                for j in range(per):
                    wait_group(buf, sems, i * per + j)
            for n, (g, k) in enumerate(spots):
                part = weights[n * ROWS : (n + 1) * ROWS] * buf[g * GROUP + k, rows].astype(F32)
                total = jnp.sum(part, axis=0, keepdims=True) * scaling
                if c == 0:
                    out_ref[g, pl.ds(k, 1), :] = total
                else:
                    out_ref[g, pl.ds(k, 1), :] += total
            return carry

        lax.fori_loop(0, groups // per, step, 0)


def pair(row):
    high, low = split(row)
    index = lax.broadcasted_iota(jnp.int32, (16, row.shape[1]), 0)
    both = jnp.where(index == 0, high.astype(F32), jnp.where(index == 1, low.astype(F32), 0.0))
    return both.astype(BF16)


def observe_kernel(which_ref, counts_ref, got_ref, innov_ref, weight_ref, tiles_ref, out_ref,
                   buf, sems):
    lon, parts, ranks, blk = got_ref.shape

    def start(s, carry):
        for r in range(ranks):
            o = jnp.maximum(which_ref[s, r], 0)
            pltpu.make_async_copy(tiles_ref.at[o], buf.at[s * ranks + r], sems.at[s]).start()
        return carry

    lax.fori_loop(0, lon, start, 0)
    lane = lax.broadcasted_iota(jnp.int32, (1, blk), 1)
    together = 2 if lon % 2 == 0 else 1

    def step(i, carry):
        todo = []
        for j in range(together):
            s = i * together + j
            view = buf.at[pl.ds(s * ranks, ranks)]
            pltpu.make_async_copy(view, view, sems.at[s]).wait()
            rows = got_ref[s, 0]
            for part in range(1, parts):
                rows = rows + got_ref[s, part]
            for r in range(ranks):
                todo.append((s, r, rows[r : r + 1]))
        seen = [
            lax.dot_general(
                pair(row), buf[s * ranks + r], (((1,), (1,)), ((), ())), preferred_element_type=F32
            )
            for s, r, row in todo
        ]
        gaps = []
        for (s, r, _), value in zip(todo, seen):
            index = which_ref[s, r]
            o = jnp.maximum(index, 0)
            count = jnp.where(index >= 0, counts_ref[o], 0)
            observed = jnp.sum(value, axis=0, keepdims=True)
            gap = weight_ref[pl.ds(o, 1), :] * (observed - innov_ref[pl.ds(o, 1), :])
            gaps.append(jnp.where(lane < count, gap, 0.0))
        for (s, r, _), gap in zip(todo, gaps):
            back = jnp.dot(pair(gap), buf[s * ranks + r], preferred_element_type=F32)
            row = jnp.sum(back, axis=0, keepdims=True)
            for part in range(parts):
                out_ref[s, part, pl.ds(r, 1), :] = row
        return carry

    lax.fori_loop(0, lon // together, step, 0)


def grad_kernel(blk, scaling, code_ref, slot_ref, adj_ref, table_ref, ctrl_ref, ens_ref, out_ref,
                low_ref, high_ref, ext, buf, sems, row_sems, out_sems):
    groups = code_ref.shape[0]
    members, nodes = ctrl_ref.shape
    chunks = members // ROWS
    copies = [
        pltpu.make_async_copy(
            ctrl_ref.at[pl.ds(i * 8, 8), :], ext.at[pl.ds(i * 8, 8), pl.ds(blk, nodes)], row_sems.at[i]
        )
        for i in range(members // 8)
    ]
    for copy in copies[: ROWS // 8]:
        copy.start()
    tile_copies(code_ref, slot_ref, ens_ref, buf, sems, blk, groups)
    for copy in copies[ROWS // 8 :]:
        copy.start()
    ext[:, :blk] = jnp.zeros((members, blk), F32)
    ext[:, nodes + blk :] = jnp.zeros((members, blk), F32)
    per = WIDE // GROUP
    writes = []
    for c in range(chunks):
        for copy in copies[c * ROWS // 8 : (c + 1) * ROWS // 8]:
            copy.wait()
        rows = slice(c * ROWS, (c + 1) * ROWS)

        def step(i, carry):
            if c == 0:
                for j in range(per):
                    wait_group(buf, sems, i * per + j)
            spots = [(i * per + j, k) for j in range(per) for k in range(GROUP)]
            pieces = []
            for g, k in spots:
                row = adj_ref[g, pl.ds(k, 1), :] * scaling
                pieces.append(buf[g * GROUP + k, rows].astype(F32) * row)
            high, low = split(jnp.concatenate(pieces, axis=0))
            both = jnp.dot(
                jnp.concatenate([high, low], axis=1), table_ref[...], preferred_element_type=F32
            )
            total = both[:, : 3 * blk] + both[:, 3 * blk :]
            for n, (g, k) in enumerate(spots):
                column = pl.multiple_of(code_ref[g, k], blk)
                ext[rows, pl.ds(column, 3 * blk)] += total[n * ROWS : (n + 1) * ROWS]
            return carry

        lax.fori_loop(0, groups // per, step, 0)
        for i in range(c * ROWS // 8, (c + 1) * ROWS // 8):
            write = pltpu.make_async_copy(
                ext.at[pl.ds(i * 8, 8), pl.ds(blk, nodes)],
                out_ref.at[pl.ds(i * 8, 8), :],
                out_sems.at[i],
            )
            write.start()
            writes.append(write)
    low_ref[...] = ext[:, :blk]
    high_ref[...] = ext[:, nodes + blk :]
    for write in writes:
        write.wait()


def edge_kernel(blk, grad_ref, before_ref, after_ref, out_ref, first, last, sems):
    nodes = grad_ref.shape[1]
    reads = [
        pltpu.make_async_copy(grad_ref.at[:, pl.ds(0, blk)], first, sems.at[0]),
        pltpu.make_async_copy(grad_ref.at[:, pl.ds(nodes - blk, blk)], last, sems.at[1]),
    ]
    for copy in reads:
        copy.start()
    for copy in reads:
        copy.wait()
    first[...] += before_ref[...]
    last[...] += after_ref[...]
    writes = [
        pltpu.make_async_copy(first, out_ref.at[:, pl.ds(0, blk)], sems.at[0]),
        pltpu.make_async_copy(last, out_ref.at[:, pl.ds(nodes - blk, blk)], sems.at[1]),
    ]
    for copy in writes:
        copy.start()
    for copy in writes:
        copy.wait()


def local(ensemble, control, obs_tiles, innovation, obs_weight, obs_counts, node_blocks, obs_slots):
    lon, mem = lax.axis_size("lon"), lax.axis_size("mem")
    obs, blk = obs_tiles.shape[0], obs_tiles.shape[2]
    members, nodes = control.shape
    nb = nodes // blk
    ranks = CAP // mem
    scaling = 1.0 / math.sqrt(members * mem - 1)
    slots = lon * CAP
    up = [(i, (i + 1) % lon) for i in range(lon)]
    down = [(j, i) for i, j in up]
    forward, backward = tables(blk)
    ens = jnp.transpose(ensemble, (1, 0, 2))
    dma = pltpu.SemaphoreType.DMA

    code, slot, which, before, after = pl.pallas_call(
        functools.partial(prepare_kernel, nb, blk, ranks),
        out_shape=(jax.ShapeDtypeStruct((lon, 128), jnp.int32),) * 3
        + (jax.ShapeDtypeStruct((members, blk), F32),) * 2,
        in_specs=[VMEM, VMEM, ANY],
        out_specs=(VMEM,) * 5,
        scratch_shapes=[pltpu.VMEM((2, members, blk), F32), dma((2,)), dma((2,))],
        compiler_params=pltpu.CompilerParams(collective_id=2, has_side_effects=True),
        name="prepare",
    )(node_blocks.reshape(lon, obs), obs_slots.reshape(lon, obs), control)

    part = pl.pallas_call(
        functools.partial(fetch_kernel, blk, scaling),
        out_shape=jax.ShapeDtypeStruct((lon, CAP, blk), F32),
        in_specs=[SMEM, SMEM, VMEM, VMEM, VMEM, ANY, ANY],
        out_specs=VMEM,
        scratch_shapes=[
            pltpu.VMEM((members, nodes + 2 * blk), F32),
            pltpu.VMEM((slots, members, blk), BF16),
            dma((lon,)),
            dma((members // 8,)),
        ],
        compiler_params=params(),
        name="fetch",
    )(code, slot, before, after, jnp.asarray(forward), control, ens)

    got = exchange(part.reshape(lon * mem, ranks, blk), 0)
    back = pl.pallas_call(
        observe_kernel,
        out_shape=jax.ShapeDtypeStruct((lon, mem, ranks, blk), F32),
        in_specs=[SMEM, SMEM, VMEM, VMEM, VMEM, ANY],
        out_specs=VMEM,
        scratch_shapes=[pltpu.VMEM((lon * ranks, blk, blk), BF16), dma((lon,))],
        compiler_params=params(),
        name="observe",
    )(which, obs_counts, got.reshape(lon, mem, ranks, blk), innovation, obs_weight, obs_tiles)
    adj = exchange(back.reshape(lon * mem, ranks, blk), 1).reshape(lon, CAP, blk)

    table = jnp.asarray(backward)
    grad, low, high = pl.pallas_call(
        functools.partial(grad_kernel, blk, scaling),
        out_shape=(jax.ShapeDtypeStruct((members, nodes), F32),)
        + (jax.ShapeDtypeStruct((members, blk), F32),) * 2,
        in_specs=[SMEM, SMEM, VMEM, VMEM, ANY, ANY],
        out_specs=(ANY, VMEM, VMEM),
        scratch_shapes=[
            pltpu.VMEM((members, nodes + 2 * blk), F32),
            pltpu.VMEM((slots, members, blk), BF16),
            dma((lon,)),
            dma((members // 8,)),
            dma((members // 8,)),
        ],
        compiler_params=params(),
        name="grad",
    )(code, slot, adj, table, control, ens)
    before = lax.ppermute(high, "lon", up)
    after = lax.ppermute(low, "lon", down)
    return pl.pallas_call(
        functools.partial(edge_kernel, blk),
        out_shape=jax.ShapeDtypeStruct((members, nodes), F32),
        in_specs=[ANY, VMEM, VMEM],
        out_specs=ANY,
        scratch_shapes=[pltpu.VMEM((members, blk), F32)] * 2 + [dma((2,))],
        input_output_aliases={0: 0},
        name="edge",
    )(grad, before, after)


def solution(mesh):
    return jax.shard_map(
        local,
        mesh=mesh,
        in_specs=(
            P("mem", None, "lon"),
            P("mem", "lon"),
            P("lon", None, None),
            P("lon", None),
            P("lon", None),
            P("lon"),
            P(),
            P(),
        ),
        out_specs=P("mem", "lon"),
        check_vma=False,
    )
```
